512 devices in a mesh: dp: 16 (over z_hi, y), tensor: 32 (over z_lo, x, core).
Axes of the slice: x: 4, y: 4, z: 16 (z_hi: 4, z_lo: 4; z = z_hi * 4 + z_lo), core: 2. Of those that a mesh axis runs over, the one named last changes fastest.
Arguments:
- hidden: bfloat16 [1024, 32, 28672], P('dp', None, 'tensor'), may hold values from -6 to 6
- out_grad: bfloat16 [1024, 32, 8192], P('dp', None, 'tensor'), may hold values from -6 to 6
- proj_in: bfloat16 [28672, 64], P('tensor'), may hold values from -0.03125 to 0.03125
- proj_out: bfloat16 [8192, 64], P('tensor'), may hold values from -0.0625 to 0.0625
- lengths: int32 [1024], P('dp'), may hold values from 1 to 32, 16384 in all
- task_ids: int32 [16], replicated, may hold values from 0 to 1
Outputs:
- similarity: float32 [1024, 16, 64], P('dp', None, 'tensor')
The draws below stay inside these ranges and needn't reach their ends.
Inputs may be any that keep to these rules, and one draw needn't show every extreme that they name: `lengths`: at least one sequence is exactly 32 long.
All inputs are finite; a program needn't handle non-finite values. No bound on the sum of `lengths` on one device may be relied on, other than what follows from the above.
Results may differ from the reference program's by a relative error of at most 0.0003.
Values sent between devices are 32-bit elements; how exact they have to be, the bound alone decides.
No kernel may reach another device: no remote copies, remote signals or barrier semaphores. Data moves between devices by JAX's collectives and lax.ppermute only.
A program may use at most 64 MiB of HBM per device.

```python
import math
import jax
import jax.numpy as jnp
import numpy as np
from jax import lax

D = 8192
FF = 28672
RANK = 64
BLOCK = 64
LEN = 32
NTASK = 2
NBLK = 16
NSEQ = 1024
N_DP = 16
N_TENSOR = 32


def touch_ends(array, stream_key, low, top_value):
    longest = array.shape.index(max(array.shape))
    spots = []
    for shift in (0, 1):
        where = [jax.random.randint(jax.random.fold_in(stream_key, axis), (), 0, length) for axis, length in enumerate(array.shape)]
        where[longest] = (where[longest] + shift) % array.shape[longest]
        spots.append(tuple(where))
    return array.at[spots[0]].set(low).at[spots[1]].set(top_value)


def block_levels(key, extent, pieces, low, largest):
    loudness = 1.0
    for position, blocks in pieces:
        steps = jax.random.uniform(jax.random.fold_in(jax.random.fold_in(key, 6), position), (blocks,), jnp.float32, low / len(pieces), largest / len(pieces))
        loudness = loudness * jnp.repeat(jnp.exp(steps), extent[position] // blocks).reshape((-1,) + (1,) * (len(extent) - 1 - position))
    return loudness


def length_profile(count, total, most, slope):
    portions = [(1 << 20) // math.isqrt(rank ** slope) + 1 for rank in range(2, count + 1)]
    spare, holding = total - most - (count - 1), [1] * (count - 1)
    while spare > 0:
        movable = [i for i in range(count - 1) if holding[i] < most]
        mass, remaining = sum([portions[i] for i in movable]), spare
        for i in movable:
            addition = min(most - holding[i], max(1, remaining * portions[i] // mass), spare)
            holding[i] = holding[i] + addition
            spare = spare - addition
    return np.array([most] + holding)


def ragged_sizes(own_key, number_of, total, most, lean):
    if number_of == 2:
        one = jax.random.randint(own_key, (), max(1, total - most), min(most, total - 1) + 1)
        return jnp.stack([one, total - one])
    sizes = jnp.asarray(length_profile(number_of, total, most, lean), jnp.int32)
    twos = (number_of - 1) // 2
    source_of, receiver = sizes[1:1 + 2 * twos:2], sizes[2:2 + 2 * twos:2]
    slack = jnp.minimum(source_of - 1, most - receiver)
    passed = jax.random.randint(jax.random.fold_in(own_key, 1), (twos,), 0, 1 << 20) % (slack + 1)
    sizes = sizes.at[1:1 + 2 * twos:2].set(source_of - passed).at[2:2 + 2 * twos:2].set(receiver + passed)
    return sizes[jax.random.permutation(jax.random.fold_in(own_key, 2), number_of)]


def scatter_about(stream_key, extent, width, most, split=(), kind=jnp.bfloat16):
    result = jax.random.normal(stream_key, extent, jnp.float32) * width
    if len(split) > 0:
        result = block_levels(stream_key, extent, split, -0.22, 0.18) * result
    return jnp.clip(result, min=-most, max=most).astype(kind)


def setup_inputs(seed: int = 0) -> dict:
    splits = jax.random.split(jax.random.key(seed), 7)
    hidden = scatter_about(splits[0], (NSEQ, LEN, FF), 1.0, 6.0, ((0, 16), (2, 32)))
    out_grad = scatter_about(splits[1], (NSEQ, LEN, D), 1.0, 6.0, ((0, 16), (2, 32)))
    proj_in = scatter_about(splits[2], (FF, RANK), FF ** -0.5, 0.03125, ((0, 32),))
    proj_out = scatter_about(splits[3], (D, RANK), D ** -0.5, 0.0625, ((0, 32),))
    lengths = ragged_sizes(splits[4], NSEQ, NSEQ * LEN // 2, LEN, 2).astype(jnp.int32)
    task_ids = touch_ends(jax.random.randint(splits[5], (NBLK,), 0, NTASK), jax.random.fold_in(splits[5], 1), 0, NTASK - 1).astype(jnp.int32)
    return {"hidden": hidden, "out_grad": out_grad, "proj_in": proj_in, "proj_out": proj_out, "lengths": lengths, "task_ids": task_ids}


epsilon = 1e-06

def normalized(summed, lengths):
    seq_count, seq_len, doubled = summed.shape
    width_low = doubled // 2
    live_mask = (jnp.arange(seq_len, dtype=jnp.int32)[None, :] < lengths[:, None]).astype(jnp.float32)
    inputs_low = summed[:, :, :width_low] * live_mask[:, :, None]
    outputs_low = summed[:, :, width_low:]
    sketch = jnp.einsum('slk,slm->skm', inputs_low, outputs_low, precision=lax.Precision.HIGHEST)
    flattened = sketch.reshape(seq_count, width_low * width_low)
    root_mean = jnp.sqrt(lax.optimization_barrier(jnp.mean(flattened * flattened, axis=1, keepdims=True)) + epsilon)
    return flattened / root_mean

def reference(hidden, out_grad, proj_in, proj_out, lengths, task_ids):
    slice_hidden = FF // N_TENSOR
    slice_model = D // N_TENSOR
    weights_in = proj_in.astype(jnp.float32).reshape(N_TENSOR, slice_hidden, RANK)
    weights_out = proj_out.astype(jnp.float32).reshape(N_TENSOR, slice_model, RANK)

    def project(operands):
        group_hidden, group_grad = operands
        acts = group_hidden.astype(jnp.float32).reshape(BLOCK * LEN, N_TENSOR, slice_hidden)
        grads = group_grad.astype(jnp.float32).reshape(BLOCK * LEN, N_TENSOR, slice_model)
        terms_in = jnp.einsum('tsf,sfr->tsr', acts, weights_in)
        terms_out = jnp.einsum('tsf,sfr->tsr', grads, weights_out)
        terms = jnp.concatenate([terms_in, terms_out], axis=2)
        return lax.optimization_barrier(jnp.sum(terms, axis=1)).reshape(BLOCK, LEN, 2 * RANK)
    grouped_hidden = hidden.reshape(N_DP, BLOCK, LEN, FF)
    grouped_grad = out_grad.reshape(N_DP, BLOCK, LEN, D)
    projected = lax.map(project, (grouped_hidden, grouped_grad)).reshape(N_DP * BLOCK, LEN, 2 * RANK)
    units = normalized(projected, lengths)
    gram = jnp.dot(units, units.T, preferred_element_type=jnp.float32, precision=lax.Precision.HIGHEST) * (1.0 / RANK)
    gram = gram.reshape(N_DP * BLOCK, N_DP, BLOCK)
    row_task = jnp.repeat(task_ids, BLOCK)
    same_task = (row_task[:, None] == task_ids[None, :])[:, :, None]
    return jnp.where(same_task, gram, jnp.float32(0.0))
```

```python
import jax
import jax.numpy as jnp
import numpy as np
from jax import lax
from jax.experimental import pallas as pl
from jax.experimental.pallas import tpu as pltpu
from jax.sharding import Mesh
from jax.sharding import PartitionSpec as P

epsilon = 1e-06

AXES = ("z_hi", "y", "z_lo", "x", "core")
SIZES = (4, 4, 4, 4, 2)
DP = ("z_hi", "y")
TENSOR = ("z_lo", "x", "core")
CHIPS = ("z_lo", "x")
ROW = ("x", "core")

HIGHEST = lax.Precision.HIGHEST
VMEM = pl.BlockSpec(memory_space=pltpu.VMEM)
SMEM = pl.BlockSpec(memory_space=pltpu.SMEM)
PROJECT_VMEM = 62 * 1024 * 1024
SMALL = pltpu.CompilerParams(vmem_limit_bytes=8 * 1024 * 1024)


def contract(left, right, dims):
    return lax.dot_general(
        left, right, (dims, ((), ())), preferred_element_type=jnp.float32, precision=HIGHEST
    )


def exchange(value, axes):
    return lax.all_to_all(value, axes, 0, 0, tiled=True)


def gather(value, axis):
    copies = jnp.broadcast_to(value[None], (lax.axis_size(axis),) + value.shape)
    return exchange(copies, axis)


def project_kernel(core_ref, hidden_ref, grad_ref, in_ref, out_ref, terms_ref):
    pairs, rows, _ = hidden_ref.shape
    rank = in_ref.shape[0]
    dims = (((1,), (1,)), ((), ()))
    hidden = hidden_ref[...].reshape(pairs * rows, -1)
    grad = grad_ref[...].reshape(pairs * rows, -1)
    left = lax.dot_general(hidden, in_ref[...], dims, preferred_element_type=jnp.float32)
    right = lax.dot_general(grad, out_ref[...], dims, preferred_element_type=jnp.float32)
    terms_ref[...] = jnp.concatenate([left, right], axis=1).reshape(pairs, rows, 2 * rank)


def project(core, hidden, grad, weights_in, weights_out, steps):
    pairs, cores, rows, wide = hidden.shape
    narrow = grad.shape[3]
    rank = weights_in.shape[0]
    block = pairs // steps
    return pl.pallas_call(
        project_kernel,
        grid_spec=pltpu.PrefetchScalarGridSpec(
            num_scalar_prefetch=1,
            grid=(steps,),
            in_specs=[
                pl.BlockSpec((block, None, rows, wide), lambda i, c: (i, c[0], 0, 0)),
                pl.BlockSpec((block, None, rows, narrow), lambda i, c: (i, c[0], 0, 0)),
                pl.BlockSpec((rank, wide), lambda i, c: (0, 0)),
                pl.BlockSpec((rank, narrow), lambda i, c: (0, 0)),
            ],
            out_specs=pl.BlockSpec((block, rows, 2 * rank), lambda i, c: (i, 0, 0)),
        ),
        out_shape=jax.ShapeDtypeStruct((pairs, rows, 2 * rank), jnp.float32),
        compiler_params=pltpu.CompilerParams(vmem_limit_bytes=PROJECT_VMEM),
        cost_estimate=pl.CostEstimate(
            flops=2 * pairs * rows * rank * (wide + narrow),
            bytes_accessed=2 * pairs * rows * (wide + narrow) + 8 * pairs * rows * rank,
            transcendentals=0,
        ),
        name="project",
    )(core, hidden, grad, weights_in, weights_out)


def sketch_kernel(place_ref, lengths_ref, terms_ref, out_ref):
    first = place_ref[0]
    total = jnp.sum(terms_ref[...], axis=0)
    share = out_ref.shape[1] // 2
    seq_len, rank = total.shape[0] // 2, total.shape[1] // 2
    slot = lax.broadcasted_iota(jnp.int32, (seq_len, rank), 0)
    for s in range(2):
        mine = total[s * seq_len : (s + 1) * seq_len]
        live = (slot < lengths_ref[first + s]).astype(jnp.float32)
        sketch = contract(mine[:, :rank] * live, mine[:, rank:], ((0,), (0,)))
        mean = jnp.sum(sketch * sketch) / (rank * rank)
        unit = sketch / jnp.sqrt(jnp.full((1, 1), mean, jnp.float32) + epsilon)
        wide = jnp.concatenate([unit[: rank // 2], unit[rank // 2 :]], axis=1)
        for j in range(out_ref.shape[0]):
            out_ref[j, s * share : (s + 1) * share, :] = wide[j * share : (j + 1) * share]


def sketches(place, lengths, terms, parts):
    rows = terms.shape[1] // (2 * parts)
    return pl.pallas_call(
        sketch_kernel,
        in_specs=[SMEM, SMEM, VMEM],
        out_specs=VMEM,
        out_shape=jax.ShapeDtypeStruct((parts, 2 * rows, terms.shape[2]), jnp.float32),
        compiler_params=SMALL,
        name="sketches",
    )(place, lengths, terms)


def gram_kernel(rows_ref, cols_ref, out_ref, held):
    share = 4
    parts, blocks, lanes = out_ref.shape
    n_rows = rows_ref.shape[0] // share
    n_cols = cols_ref.shape[0] // (2 * share)
    halves = [jnp.zeros((n_cols, n_rows), jnp.float32) for _ in range(2)]
    for r in range(share):
        right = rows_ref[pl.ds(r, n_rows, stride=share), :]
        for s in range(2):
            left = cols_ref[pl.ds(s * share + r, n_cols, stride=2 * share), :]
            halves[s] = halves[s] + contract(left, right, ((1,), (1,)))
    held[...] = jnp.concatenate(halves, axis=1)
    for d in range(parts):
        out_ref[d] = held[pl.ds(d, blocks, stride=parts), :]


def gram(rows, cols, parts, blocks):
    lanes = 2 * (rows.shape[0] // 4)
    return pl.pallas_call(
        gram_kernel,
        in_specs=[VMEM, VMEM],
        out_specs=VMEM,
        out_shape=jax.ShapeDtypeStruct((parts, blocks, lanes), jnp.float32),
        scratch_shapes=[pltpu.VMEM((parts * blocks, lanes), jnp.float32)],
        compiler_params=SMALL,
        name="gram",
    )(rows, cols)


def finish_kernel(place_ref, tasks_ref, terms_ref, out_ref):
    group = place_ref[0]
    z_own = place_ref[1]
    n_y, n_z, seqs = 4, 4, out_ref.shape[2]
    total = jnp.sum(terms_ref[...], axis=0) * (1.0 / seqs)
    for y in range(n_y):
        for k in range(n_z):
            z = (z_own + n_z - k) % n_z
            block = z * n_y + y
            same = tasks_ref[block] == tasks_ref[group]
            row = total[y * n_z + k : y * n_z + k + 1]
            row = jnp.where(same, row, jnp.float32(0.0))
            out_ref[block] = jnp.concatenate([row[:, :seqs], row[:, seqs:]], axis=0)


def finish(place, tasks, terms):
    _, groups, lanes = terms.shape
    return pl.pallas_call(
        finish_kernel,
        in_specs=[SMEM, SMEM, VMEM],
        out_specs=VMEM,
        out_shape=jax.ShapeDtypeStruct((groups, 2, lanes // 2), jnp.float32),
        compiler_params=SMALL,
        name="finish",
    )(place, tasks, terms)


def body(hidden, out_grad, proj_in, proj_out, lengths, task_ids):
    block_rows, seq_len, _ = hidden.shape
    rank = proj_in.shape[1]
    groups = lax.axis_size(DP)
    parts = lax.axis_size(ROW)
    chips = lax.axis_size(CHIPS)
    share = block_rows // lax.axis_size(TENSOR)
    pair_rows = share * seq_len
    core = lax.axis_index("core")
    slice_index = lax.axis_index(TENSOR)
    group_index = lax.axis_index(DP)

    hidden = hidden.reshape(chips, 2, pair_rows, -1)
    out_grad = out_grad.reshape(chips, 2, pair_rows, -1)
    own = jnp.reshape(core, (1,)).astype(jnp.int32)
    weights = (proj_in.T, proj_out.T)
    send = project(1 - own, hidden, out_grad, *weights, 2)
    keep = project(own, hidden, out_grad, *weights, 2)
    mine = keep + lax.ppermute(send, "core", [(0, 1), (1, 0)])
    terms = exchange(mine, CHIPS)
    place = jnp.reshape(slice_index * share, (1,)).astype(jnp.int32)
    units = sketches(place, lengths, terms, parts)
    entries = exchange(units, ROW).reshape(-1, 2 * rank)
    n_z = lax.axis_size("z_hi")
    far = [entries]
    for k in range(1, n_z):
        far.append(lax.ppermute(entries, "z_hi", [(i, (i + k) % n_z) for i in range(n_z)]))
    rows = gather(entries, "z_lo").reshape(-1, 2 * rank)
    cols = gather(jnp.stack(far), "y").reshape(-1, 2 * rank)
    partial_value = gram(rows, cols, parts, groups)
    place = jnp.stack([group_index, lax.axis_index("z_hi")]).astype(jnp.int32)
    return finish(place, task_ids, exchange(partial_value, ROW)).transpose(2, 0, 1)


def solution(mesh):
    fine = Mesh(np.asarray(mesh.devices).reshape(SIZES), AXES)
    in_specs = (
        P(DP, None, TENSOR),
        P(DP, None, TENSOR),
        P(TENSOR, None),
        P(TENSOR, None),
        P(DP),
        P(),
    )
    out_specs = P(DP, None, TENSOR)
    return jax.shard_map(body, mesh=fine, in_specs=in_specs, out_specs=out_specs, check_vma=False)
```

```python
import functools

import jax
import jax.numpy as jnp
import numpy as np
from jax import lax
from jax.experimental import pallas as pl
from jax.experimental.pallas import tpu as pltpu
from jax.sharding import Mesh
from jax.sharding import PartitionSpec as P

epsilon = 1e-06

AXES = ("z_hi", "y", "z_lo", "x", "core")
SIZES = (4, 4, 4, 4, 2)
DP = ("z_hi", "y")
TENSOR = ("z_lo", "x", "core")
CHIPS = ("z_lo", "x")

HIGHEST = lax.Precision.HIGHEST
VMEM = pl.BlockSpec(memory_space=pltpu.VMEM)
SMEM = pl.BlockSpec(memory_space=pltpu.SMEM)
CHUNKS = 4
HBM = pl.BlockSpec(memory_space=pltpu.HBM)
SMALL = pltpu.CompilerParams(vmem_limit_bytes=8 * 1024 * 1024)


def contract(left, right, dims):
    return lax.dot_general(
        left, right, (dims, ((), ())), preferred_element_type=jnp.float32, precision=HIGHEST
    )


def exchange(value, axes):
    return lax.all_to_all(value, axes, 0, 0, tiled=True)


def gather(value, axis):
    copies = jnp.broadcast_to(value[None], (lax.axis_size(axis),) + value.shape)
    return exchange(copies, axis)


def project_kernel(away, hidden_hbm, grad_hbm, in_hbm, out_hbm, terms_ref, hidden, grad, w_in, w_out, sems):
    core = lax.axis_index("core")
    core = 1 - core if away else core
    pairs, rows, lanes = terms_ref.shape
    block = pairs // CHUNKS
    dims = (((1,), (1,)), ((), ()))
    weights = [
        pltpu.make_async_copy(in_hbm, w_in, sems.at[0, CHUNKS]),
        pltpu.make_async_copy(out_hbm, w_out, sems.at[1, CHUNKS]),
    ]
    for copy in weights:
        copy.start()
    chunks = []
    for j in range(CHUNKS):
        span = pl.ds(j * block, block)
        chunks.append(
            [
                pltpu.make_async_copy(hidden_hbm.at[span, core], hidden.at[span], sems.at[0, j]),
                pltpu.make_async_copy(grad_hbm.at[span, core], grad.at[span], sems.at[1, j]),
            ]
        )
        for copy in chunks[-1]:
            copy.start()
    for copy in weights:
        copy.wait()
    for j in range(CHUNKS):
        for copy in chunks[j]:
            copy.wait()
        span = slice(j * block, (j + 1) * block)
        acts = hidden[span].reshape(block * rows, -1)
        grads = grad[span].reshape(block * rows, -1)
        left = lax.dot_general(acts, w_in[...], dims, preferred_element_type=jnp.float32)
        right = lax.dot_general(grads, w_out[...], dims, preferred_element_type=jnp.float32)
        terms_ref[span] = jnp.concatenate([left, right], axis=1).reshape(block, rows, lanes)


def project(away, hidden, grad, weights_in, weights_out):
    pairs, _, rows, wide = hidden.shape
    narrow = grad.shape[3]
    rank = weights_in.shape[0]
    operands = (hidden, grad, weights_in, weights_out)
    return pl.pallas_call(
        functools.partial(project_kernel, away),
        in_specs=[HBM, HBM, HBM, HBM],
        out_specs=VMEM,
        out_shape=jax.ShapeDtypeStruct((pairs, rows, 2 * rank), jnp.float32),
        scratch_shapes=[
            pltpu.VMEM((pairs, rows, wide), hidden.dtype),
            pltpu.VMEM((pairs, rows, narrow), grad.dtype),
            pltpu.VMEM(weights_in.shape, weights_in.dtype),
            pltpu.VMEM(weights_out.shape, weights_out.dtype),
            pltpu.SemaphoreType.DMA((2, CHUNKS + 1)),
        ],
        compiler_params=pltpu.CompilerParams(vmem_limit_bytes=16 * 1024 * 1024),
        cost_estimate=pl.CostEstimate(
            flops=2 * pairs * rows * rank * (wide + narrow),
            bytes_accessed=2 * pairs * rows * (wide + narrow) + 8 * pairs * rows * rank,
            transcendentals=0,
        ),
        name="project",
    )(*(pltpu.with_memory_space_constraint(v, pltpu.HBM) for v in operands))


def add_kernel(left_ref, right_ref, out_ref):
    out_ref[...] = left_ref[...] + right_ref[...]


def add(left, right):
    return pl.pallas_call(
        add_kernel,
        in_specs=[VMEM, VMEM],
        out_specs=VMEM,
        out_shape=jax.ShapeDtypeStruct(left.shape, left.dtype),
        compiler_params=SMALL,
        name="add",
    )(left, right)


def sketch_kernel(lengths_ref, terms_ref, out_ref):
    first = 2 * lax.axis_index(TENSOR)
    total = jnp.sum(terms_ref[...], axis=0)
    share = out_ref.shape[1] // 2
    parts = terms_ref.shape[0]
    copies = out_ref.shape[0] // parts
    seq_len, rank = total.shape[0] // 2, total.shape[1] // 2
    slot = lax.broadcasted_iota(jnp.int32, (seq_len, rank), 0)
    for s in range(2):
        mine = total[s * seq_len : (s + 1) * seq_len]
        live = (slot < lengths_ref[first + s]).astype(jnp.float32)
        sketch = contract(mine[:, :rank] * live, mine[:, rank:], ((0,), (0,)))
        mean = jnp.sum(sketch * sketch) / (rank * rank)
        unit = sketch / jnp.sqrt(jnp.full((1, 1), mean, jnp.float32) + epsilon)
        wide = jnp.concatenate([unit[: rank // 2], unit[rank // 2 :]], axis=1)
        for j in range(parts):
            piece = wide[j * share : (j + 1) * share]
            for k in range(copies):
                out_ref[k * parts + j, s * share : (s + 1) * share, :] = piece


def sketches(lengths, terms, copies):
    parts, slots, lanes = terms.shape
    rows = slots // (2 * parts)
    return pl.pallas_call(
        sketch_kernel,
        in_specs=[SMEM, VMEM],
        out_specs=VMEM,
        out_shape=jax.ShapeDtypeStruct((copies * parts, 2 * rows, lanes), jnp.float32),
        compiler_params=SMALL,
        name="sketches",
    )(lengths, terms)


def gram_kernel(own_ref, other_ref, cols_ref, out_ref, rows, held):
    parts, blocks, lanes = out_ref.shape
    share = rows.shape[0]
    first = lax.axis_index("core") == 0
    own, other = own_ref[...], other_ref[...]
    held[0] = jnp.where(first, own, other)
    held[1] = jnp.where(first, other, own)
    for core in range(2):
        for s in range(2):
            for r in range(share):
                rows[r, pl.ds(2 * core + s, parts, stride=4), :] = held[
                    core, pl.ds(s * share + r, parts, stride=2 * share), :
                ]
    halves = []
    for s in range(2):
        total = jnp.zeros((parts * blocks, lanes // 2), jnp.float32)
        for r in range(share):
            left = cols_ref[pl.ds(s * share + r, parts * blocks, stride=2 * share), :]
            total = total + contract(left, rows[r], ((1,), (1,)))
        halves.append(total)
    both = jnp.concatenate(halves, axis=1).reshape(blocks, parts, lanes)
    for b in range(blocks):
        out_ref[:, b, :] = both[b]


def gram(own, other, cols, parts, blocks):
    n_slots, lanes = own.shape
    share = n_slots // (2 * parts)
    return pl.pallas_call(
        gram_kernel,
        in_specs=[VMEM, VMEM, VMEM],
        out_specs=VMEM,
        out_shape=jax.ShapeDtypeStruct((parts, blocks, 2 * 4 * parts), jnp.float32),
        scratch_shapes=[
            pltpu.VMEM((share, 4 * parts, lanes), jnp.float32),
            pltpu.VMEM((2, n_slots, lanes), jnp.float32),
        ],
        compiler_params=SMALL,
        name="gram",
    )(own, other, cols)


def finish_kernel(tasks_ref, terms_ref, out_ref):
    group = lax.axis_index(DP)
    n_y, n_z, seqs = 4, 4, out_ref.shape[2]
    total = jnp.sum(terms_ref[...], axis=0) * (1.0 / seqs)
    for y in range(n_y):
        for k in range(n_z):
            z = k
            block = z * n_y + y
            same = tasks_ref[block] == tasks_ref[group]
            row = total[y * n_z + k : y * n_z + k + 1]
            row = jnp.where(same, row, jnp.float32(0.0))
            out_ref[block] = jnp.concatenate([row[:, :seqs], row[:, seqs:]], axis=0)


def finish(tasks, terms):
    _, groups, lanes = terms.shape
    return pl.pallas_call(
        finish_kernel,
        in_specs=[SMEM, VMEM],
        out_specs=VMEM,
        out_shape=jax.ShapeDtypeStruct((groups, 2, lanes // 2), jnp.float32),
        compiler_params=SMALL,
        name="finish",
    )(tasks, terms)


def body(hidden, out_grad, proj_in, proj_out, lengths, task_ids):
    block_rows, seq_len, _ = hidden.shape
    rank = proj_in.shape[1]
    groups = lax.axis_size(DP)
    chips = lax.axis_size(CHIPS)
    share = block_rows // lax.axis_size(TENSOR)
    pair_rows = share * seq_len

    hidden = hidden.reshape(chips, 2, pair_rows, -1)
    out_grad = out_grad.reshape(chips, 2, pair_rows, -1)
    weights = (proj_in.T, proj_out.T)
    send = project(True, hidden, out_grad, *weights)
    keep = project(False, hidden, out_grad, *weights)
    mine = add(keep, lax.ppermute(send, "core", [(0, 1), (1, 0)]))
    terms = exchange(mine, CHIPS)
    n_z = lax.axis_size("z_hi")
    units = sketches(lengths, terms, n_z)
    spread = exchange(units, ("z_hi",) + CHIPS).reshape(n_z, -1, 2 * rank)
    mine = lax.dynamic_index_in_dim(spread, lax.axis_index("z_hi"), 0, keepdims=False)
    other = lax.ppermute(mine, "core", [(0, 1), (1, 0)])
    cols = gather(spread, "y").reshape(-1, 2 * rank)
    partial_value = gram(mine, other, cols, chips, groups)
    return finish(task_ids, exchange(partial_value, CHIPS)).transpose(2, 0, 1)


def solution(mesh):
    fine = Mesh(np.asarray(mesh.devices).reshape(SIZES), AXES)
    in_specs = (
        P(DP, None, TENSOR),
        P(DP, None, TENSOR),
        P(TENSOR, None),
        P(TENSOR, None),
        P(DP),
        P(),
    )
    out_specs = P(DP, None, TENSOR)
    return jax.shard_map(body, mesh=fine, in_specs=in_specs, out_specs=out_specs, check_vma=False)
```

```python
import jax
import jax.numpy as jnp
import numpy as np
from jax import lax
from jax.experimental import pallas as pl
from jax.experimental.pallas import tpu as pltpu
from jax.sharding import Mesh
from jax.sharding import PartitionSpec as P

epsilon = 1e-06

AXES = ("z_hi", "y", "z_lo", "x", "core")
SIZES = (4, 4, 4, 4, 2)
DP = ("z_hi", "y")
TENSOR = ("z_lo", "x", "core")
CHIPS = ("z_lo", "x")

HIGHEST = lax.Precision.HIGHEST
VMEM = pl.BlockSpec(memory_space=pltpu.VMEM)
CHUNKS = 4
HBM = pl.BlockSpec(memory_space=pltpu.HBM)
SMALL = pltpu.CompilerParams(vmem_limit_bytes=8 * 1024 * 1024)


def contract(left, right, dims):
    return lax.dot_general(
        left, right, (dims, ((), ())), preferred_element_type=jnp.float32, precision=HIGHEST
    )


def exchange(value, axes):
    return lax.all_to_all(value, axes, 0, 0, tiled=True)


def gather(value, axis):
    copies = jnp.broadcast_to(value[None], (lax.axis_size(axis),) + value.shape)
    return exchange(copies, axis)


def project_kernel(hidden_hbm, grad_hbm, in_hbm, out_hbm, terms_ref, hidden, grad, w_in, w_out, sems):
    core = 1 - lax.axis_index("core")
    pairs, rows, lanes = terms_ref.shape
    block = pairs // CHUNKS
    dims = (((1,), (1,)), ((), ()))
    weights = [
        pltpu.make_async_copy(in_hbm, w_in, sems.at[0, CHUNKS]),
        pltpu.make_async_copy(out_hbm, w_out, sems.at[1, CHUNKS]),
    ]
    for copy in weights:
        copy.start()
    chunks = []
    for j in range(CHUNKS):
        span = pl.ds(j * block, block)
        chunks.append(
            [
                pltpu.make_async_copy(hidden_hbm.at[span, core], hidden.at[span], sems.at[0, j]),
                pltpu.make_async_copy(grad_hbm.at[span, core], grad.at[span], sems.at[1, j]),
            ]
        )
        for copy in chunks[-1]:
            copy.start()
    for copy in weights:
        copy.wait()
    for j in range(CHUNKS):
        for copy in chunks[j]:
            copy.wait()
        span = slice(j * block, (j + 1) * block)
        acts = hidden[span].reshape(block * rows, -1)
        grads = grad[span].reshape(block * rows, -1)
        left = lax.dot_general(acts, w_in[...], dims, preferred_element_type=jnp.float32)
        right = lax.dot_general(grads, w_out[...], dims, preferred_element_type=jnp.float32)
        terms_ref[span] = jnp.concatenate([left, right], axis=1).reshape(block, rows, lanes)


def project(hidden, grad, weights_in, weights_out):
    pairs, _, rows, wide = hidden.shape
    narrow = grad.shape[3]
    rank = weights_in.shape[0]
    operands = (hidden, grad, weights_in, weights_out)
    return pl.pallas_call(
        project_kernel,
        in_specs=[HBM, HBM, HBM, HBM],
        out_specs=VMEM,
        out_shape=jax.ShapeDtypeStruct((pairs, rows, 2 * rank), jnp.float32),
        scratch_shapes=[
            pltpu.VMEM((pairs, rows, wide), hidden.dtype),
            pltpu.VMEM((pairs, rows, narrow), grad.dtype),
            pltpu.VMEM(weights_in.shape, weights_in.dtype),
            pltpu.VMEM(weights_out.shape, weights_out.dtype),
            pltpu.SemaphoreType.DMA((2, CHUNKS + 1)),
        ],
        compiler_params=pltpu.CompilerParams(vmem_limit_bytes=16 * 1024 * 1024),
        cost_estimate=pl.CostEstimate(
            flops=2 * pairs * rows * rank * (wide + narrow),
            bytes_accessed=2 * pairs * rows * (wide + narrow) + 8 * pairs * rows * rank,
            transcendentals=0,
        ),
        name="project",
    )(*(pltpu.with_memory_space_constraint(v, pltpu.HBM) for v in operands))


def rest_kernel(hidden_ref, grad_ref, in_ref, out_ref, terms_ref):
    core = lax.axis_index("core")
    pairs, rows, lanes = terms_ref.shape
    block = pairs // CHUNKS
    dims = (((1,), (1,)), ((), ()))
    for j in range(CHUNKS):
        span = slice(j * block, (j + 1) * block)
        acts = hidden_ref[span, core].reshape(block * rows, -1)
        grads = grad_ref[span, core].reshape(block * rows, -1)
        left = lax.dot_general(acts, in_ref[...], dims, preferred_element_type=jnp.float32)
        right = lax.dot_general(grads, out_ref[...], dims, preferred_element_type=jnp.float32)
        terms_ref[span] = jnp.concatenate([left, right], axis=1).reshape(block, rows, lanes)


def project_rest(hidden, grad, weights_in, weights_out):
    pairs, _, rows, wide = hidden.shape
    rank = weights_in.shape[0]
    return pl.pallas_call(
        rest_kernel,
        in_specs=[VMEM, VMEM, VMEM, VMEM],
        out_specs=VMEM,
        out_shape=jax.ShapeDtypeStruct((pairs, rows, 2 * rank), jnp.float32),
        compiler_params=pltpu.CompilerParams(vmem_limit_bytes=16 * 1024 * 1024),
        cost_estimate=pl.CostEstimate(
            flops=2 * pairs * rows * rank * (wide + grad.shape[3]),
            bytes_accessed=8 * pairs * rows * rank,
            transcendentals=0,
        ),
        name="project_rest",
    )(hidden, grad, weights_in, weights_out)


def add_kernel(left_ref, right_ref, out_ref):
    out_ref[...] = left_ref[...] + right_ref[...]


def add(left, right):
    return pl.pallas_call(
        add_kernel,
        in_specs=[VMEM, VMEM],
        out_specs=VMEM,
        out_shape=jax.ShapeDtypeStruct(left.shape, left.dtype),
        compiler_params=SMALL,
        name="add",
    )(left, right)


def sketch_kernel(lengths_ref, terms_ref, out_ref):
    first = 2 * lax.axis_index(TENSOR)
    total = jnp.sum(terms_ref[...], axis=0)
    share = out_ref.shape[1] // 2
    parts = terms_ref.shape[0]
    copies = out_ref.shape[0] // parts
    seq_len, rank = total.shape[0] // 2, total.shape[1] // 2
    slot = lax.broadcasted_iota(jnp.int32, (seq_len, rank), 0)
    lengths = lengths_ref[...]
    lane = lax.broadcasted_iota(jnp.int32, lengths.shape, 1)
    for s in range(2):
        mine = total[s * seq_len : (s + 1) * seq_len]
        length = jnp.sum(jnp.where(lane == first + s, lengths, 0), axis=1, keepdims=True)
        live = (slot < length).astype(jnp.float32)
        sketch = contract(mine[:, :rank] * live, mine[:, rank:], ((0,), (0,)))
        mean = jnp.sum(sketch * sketch) / (rank * rank)
        unit = sketch / jnp.sqrt(jnp.full((1, 1), mean, jnp.float32) + epsilon)
        wide = jnp.concatenate([unit[: rank // 2], unit[rank // 2 :]], axis=1)
        for j in range(parts):
            piece = wide[j * share : (j + 1) * share]
            for k in range(copies):
                out_ref[k * parts + j, s * share : (s + 1) * share, :] = piece


def sketches(lengths, terms, copies):
    parts, slots, lanes = terms.shape
    rows = slots // (2 * parts)
    return pl.pallas_call(
        sketch_kernel,
        in_specs=[VMEM, VMEM],
        out_specs=VMEM,
        out_shape=jax.ShapeDtypeStruct((copies * parts, 2 * rows, lanes), jnp.float32),
        compiler_params=SMALL,
        name="sketches",
    )(lengths[None], terms)


def gram_kernel(own_ref, other_ref, cols_ref, out_ref, rows, held):
    parts, blocks, lanes = out_ref.shape
    share = rows.shape[0]
    first = lax.axis_index("core") == 0
    own, other = own_ref[...], other_ref[...]
    held[0] = jnp.where(first, own, other)
    held[1] = jnp.where(first, other, own)
    for core in range(2):
        for s in range(2):
            for r in range(share):
                rows[r, pl.ds(2 * core + s, parts, stride=4), :] = held[
                    core, pl.ds(s * share + r, parts, stride=2 * share), :
                ]
    halves = []
    for s in range(2):
        total = jnp.zeros((parts * blocks, lanes // 2), jnp.float32)
        for r in range(share):
            left = cols_ref[pl.ds(s * share + r, parts * blocks, stride=2 * share), :]
            total = total + contract(left, rows[r], ((1,), (1,)))
        halves.append(total)
    both = jnp.concatenate(halves, axis=1).reshape(blocks, parts, lanes)
    for b in range(blocks):
        out_ref[:, b, :] = both[b]


def gram(own, other, cols, parts, blocks):
    n_slots, lanes = own.shape
    share = n_slots // (2 * parts)
    return pl.pallas_call(
        gram_kernel,
        in_specs=[VMEM, VMEM, VMEM],
        out_specs=VMEM,
        out_shape=jax.ShapeDtypeStruct((parts, blocks, 2 * 4 * parts), jnp.float32),
        scratch_shapes=[
            pltpu.VMEM((share, 4 * parts, lanes), jnp.float32),
            pltpu.VMEM((2, n_slots, lanes), jnp.float32),
        ],
        compiler_params=SMALL,
        name="gram",
    )(own, other, cols)


def finish_kernel(tasks_ref, terms_ref, out_ref):
    group = lax.axis_index(DP)
    n_y, n_z, seqs = 4, 4, out_ref.shape[2]
    total = jnp.sum(terms_ref[...], axis=0) * (1.0 / seqs)
    tasks = tasks_ref[...]
    lane = lax.broadcasted_iota(jnp.int32, tasks.shape, 1)
    own = jnp.sum(jnp.where(lane == group, tasks, 0), axis=1, keepdims=True)
    same = jnp.where(tasks == own, 1.0, 0.0)
    blocks = out_ref.shape[0]
    row = lax.broadcasted_iota(jnp.int32, (blocks, blocks), 0)
    col = lax.broadcasted_iota(jnp.int32, (blocks, blocks), 1)
    hit = row % n_z * n_y + row // n_z == col
    live = jnp.sum(jnp.where(hit, jnp.broadcast_to(same, (blocks, blocks)), 0.0), axis=1, keepdims=True)
    total = jnp.where(live > 0.5, total, 0.0)
    for y in range(n_y):
        for z in range(n_z):
            line = total[y * n_z + z : y * n_z + z + 1]
            out_ref[z * n_y + y] = jnp.concatenate([line[:, :seqs], line[:, seqs:]], axis=0)


def finish(tasks, terms):
    _, groups, lanes = terms.shape
    return pl.pallas_call(
        finish_kernel,
        in_specs=[VMEM, VMEM],
        out_specs=VMEM,
        out_shape=jax.ShapeDtypeStruct((groups, 2, lanes // 2), jnp.float32),
        compiler_params=SMALL,
        name="finish",
    )(tasks[None], terms)


def body(hidden, out_grad, proj_in, proj_out, lengths, task_ids):
    block_rows, seq_len, _ = hidden.shape
    rank = proj_in.shape[1]
    groups = lax.axis_size(DP)
    chips = lax.axis_size(CHIPS)
    share = block_rows // lax.axis_size(TENSOR)
    pair_rows = share * seq_len

    hidden = hidden.reshape(chips, 2, pair_rows, -1)
    out_grad = out_grad.reshape(chips, 2, pair_rows, -1)
    weights = (proj_in.T, proj_out.T)
    send = project(hidden, out_grad, *weights)
    keep = project_rest(hidden, out_grad, *weights)
    mine = add(keep, lax.ppermute(send, "core", [(0, 1), (1, 0)]))
    terms = exchange(mine, CHIPS)
    n_z = lax.axis_size("z_hi")
    units = sketches(lengths, terms, n_z)
    spread = exchange(units, ("z_hi",) + CHIPS).reshape(n_z, -1, 2 * rank)
    mine = lax.dynamic_index_in_dim(spread, lax.axis_index("z_hi"), 0, keepdims=False)
    other = lax.ppermute(mine, "core", [(0, 1), (1, 0)])
    cols = gather(spread, "y").reshape(-1, 2 * rank)
    partial_value = gram(mine, other, cols, chips, groups)
    return finish(task_ids, exchange(partial_value, CHIPS)).transpose(2, 0, 1)


def solution(mesh):
    fine = Mesh(np.asarray(mesh.devices).reshape(SIZES), AXES)
    in_specs = (
        P(DP, None, TENSOR),
        P(DP, None, TENSOR),
        P(TENSOR, None),
        P(TENSOR, None),
        P(DP),
        P(),
    )
    out_specs = P(DP, None, TENSOR)
    return jax.shard_map(body, mesh=fine, in_specs=in_specs, out_specs=out_specs, check_vma=False)
```

```python
import jax
import jax.numpy as jnp
import numpy as np
from jax import lax
from jax.experimental import pallas as pl
from jax.experimental.pallas import tpu as pltpu
from jax.sharding import Mesh
from jax.sharding import PartitionSpec as P

epsilon = 1e-06

AXES = ("z_hi", "y", "z_lo", "x", "core")
SIZES = (4, 4, 4, 4, 2)
DP = ("z_hi", "y")
TENSOR = ("z_lo", "x", "core")
CHIPS = ("z_lo", "x")

HIGHEST = lax.Precision.HIGHEST
VMEM = pl.BlockSpec(memory_space=pltpu.VMEM)
CHUNKS = 2
HBM = pl.BlockSpec(memory_space=pltpu.HBM)
SMALL = pltpu.CompilerParams(vmem_limit_bytes=8 * 1024 * 1024)


def contract(left, right, dims):
    return lax.dot_general(
        left, right, (dims, ((), ())), preferred_element_type=jnp.float32, precision=HIGHEST
    )


def exchange(value, axes):
    return lax.all_to_all(value, axes, 0, 0, tiled=True)


def gather(value, axis):
    copies = jnp.broadcast_to(value[None], (lax.axis_size(axis),) + value.shape)
    return exchange(copies, axis)


def project_kernel(hidden_hbm, grad_hbm, in_hbm, out_hbm, terms_ref, hidden, grad, w_in, w_out, sems):
    core = 1 - lax.axis_index("core")
    pairs, rows, lanes = terms_ref.shape
    block = pairs // CHUNKS
    dims = (((1,), (1,)), ((), ()))
    weights = [
        pltpu.make_async_copy(in_hbm, w_in, sems.at[0, CHUNKS]),
        pltpu.make_async_copy(out_hbm, w_out, sems.at[1, CHUNKS]),
    ]
    for copy in weights:
        copy.start()
    chunks = []
    for j in range(CHUNKS):
        span = pl.ds(j * block, block)
        chunks.append(
            [
                pltpu.make_async_copy(hidden_hbm.at[span, core], hidden.at[span], sems.at[0, j]),
                pltpu.make_async_copy(grad_hbm.at[span, core], grad.at[span], sems.at[1, j]),
            ]
        )
        for copy in chunks[-1]:
            copy.start()
    for copy in weights:
        copy.wait()
    for j in range(CHUNKS):
        for copy in chunks[j]:
            copy.wait()
        span = slice(j * block, (j + 1) * block)
        acts = hidden[span].reshape(block * rows, -1)
        grads = grad[span].reshape(block * rows, -1)
        left = lax.dot_general(acts, w_in[...], dims, preferred_element_type=jnp.float32)
        right = lax.dot_general(grads, w_out[...], dims, preferred_element_type=jnp.float32)
        terms_ref[span] = jnp.concatenate([left, right], axis=1).reshape(block, rows, lanes)


def project(hidden, grad, weights_in, weights_out):
    pairs, _, rows, wide = hidden.shape
    narrow = grad.shape[3]
    rank = weights_in.shape[0]
    operands = (hidden, grad, weights_in, weights_out)
    return pl.pallas_call(
        project_kernel,
        in_specs=[HBM, HBM, HBM, HBM],
        out_specs=VMEM,
        out_shape=jax.ShapeDtypeStruct((pairs, rows, 2 * rank), jnp.float32),
        scratch_shapes=[
            pltpu.VMEM((pairs, rows, wide), hidden.dtype),
            pltpu.VMEM((pairs, rows, narrow), grad.dtype),
            pltpu.VMEM(weights_in.shape, weights_in.dtype),
            pltpu.VMEM(weights_out.shape, weights_out.dtype),
            pltpu.SemaphoreType.DMA((2, CHUNKS + 1)),
        ],
        compiler_params=pltpu.CompilerParams(vmem_limit_bytes=16 * 1024 * 1024),
        cost_estimate=pl.CostEstimate(
            flops=2 * pairs * rows * rank * (wide + narrow),
            bytes_accessed=2 * pairs * rows * (wide + narrow) + 8 * pairs * rows * rank,
            transcendentals=0,
        ),
        name="project",
    )(*(pltpu.with_memory_space_constraint(v, pltpu.HBM) for v in operands))


def rest_kernel(hidden_ref, grad_ref, in_ref, out_ref, terms_ref):
    core = lax.axis_index("core")
    pairs, rows, lanes = terms_ref.shape
    block = pairs // CHUNKS
    dims = (((1,), (1,)), ((), ()))
    for j in range(CHUNKS):
        span = slice(j * block, (j + 1) * block)
        acts = hidden_ref[span, core].reshape(block * rows, -1)
        grads = grad_ref[span, core].reshape(block * rows, -1)
        left = lax.dot_general(acts, in_ref[...], dims, preferred_element_type=jnp.float32)
        right = lax.dot_general(grads, out_ref[...], dims, preferred_element_type=jnp.float32)
        terms_ref[span] = jnp.concatenate([left, right], axis=1).reshape(block, rows, lanes)


def project_rest(hidden, grad, weights_in, weights_out):
    pairs, _, rows, wide = hidden.shape
    rank = weights_in.shape[0]
    return pl.pallas_call(
        rest_kernel,
        in_specs=[VMEM, VMEM, VMEM, VMEM],
        out_specs=VMEM,
        out_shape=jax.ShapeDtypeStruct((pairs, rows, 2 * rank), jnp.float32),
        compiler_params=pltpu.CompilerParams(vmem_limit_bytes=16 * 1024 * 1024),
        cost_estimate=pl.CostEstimate(
            flops=2 * pairs * rows * rank * (wide + grad.shape[3]),
            bytes_accessed=8 * pairs * rows * rank,
            transcendentals=0,
        ),
        name="project_rest",
    )(hidden, grad, weights_in, weights_out)


def add_kernel(left_ref, right_ref, out_ref):
    out_ref[...] = left_ref[...] + right_ref[...]


def add(left, right):
    return pl.pallas_call(
        add_kernel,
        in_specs=[VMEM, VMEM],
        out_specs=VMEM,
        out_shape=jax.ShapeDtypeStruct(left.shape, left.dtype),
        compiler_params=SMALL,
        name="add",
    )(left, right)


def sketch_kernel(lengths_ref, terms_ref, out_ref):
    first = 2 * lax.axis_index(TENSOR)
    total = jnp.sum(terms_ref[...], axis=0)
    share = out_ref.shape[1] // 2
    parts = terms_ref.shape[0]
    copies = out_ref.shape[0] // parts
    seq_len, rank = total.shape[0] // 2, total.shape[1] // 2
    slot = lax.broadcasted_iota(jnp.int32, (seq_len, rank), 0)
    lengths = lengths_ref[...]
    lane = lax.broadcasted_iota(jnp.int32, lengths.shape, 1)
    for s in range(2):
        mine = total[s * seq_len : (s + 1) * seq_len]
        length = jnp.sum(jnp.where(lane == first + s, lengths, 0), axis=1, keepdims=True)
        live = (slot < length).astype(jnp.float32)
        sketch = contract(mine[:, :rank] * live, mine[:, rank:], ((0,), (0,)))
        mean = jnp.sum(sketch * sketch) / (rank * rank)
        unit = sketch / jnp.sqrt(jnp.full((1, 1), mean, jnp.float32) + epsilon)
        wide = jnp.concatenate([unit[: rank // 2], unit[rank // 2 :]], axis=1)
        for j in range(parts):
            piece = wide[j * share : (j + 1) * share]
            for k in range(copies):
                out_ref[k * parts + j, s * share : (s + 1) * share, :] = piece


def sketches(lengths, terms, copies):
    parts, slots, lanes = terms.shape
    rows = slots // (2 * parts)
    return pl.pallas_call(
        sketch_kernel,
        in_specs=[VMEM, VMEM],
        out_specs=VMEM,
        out_shape=jax.ShapeDtypeStruct((copies * parts, 2 * rows, lanes), jnp.float32),
        compiler_params=SMALL,
        name="sketches",
    )(lengths[None], terms)


def gram_kernel(own_ref, other_ref, cols_ref, out_ref, rows, held):
    parts, blocks, lanes = out_ref.shape
    share = rows.shape[0]
    first = lax.axis_index("core") == 0
    own, other = own_ref[...], other_ref[...]
    held[0] = jnp.where(first, own, other)
    held[1] = jnp.where(first, other, own)
    for core in range(2):
        for s in range(2):
            for r in range(share):
                rows[r, pl.ds(2 * core + s, parts, stride=4), :] = held[
                    core, pl.ds(s * share + r, parts, stride=2 * share), :
                ]
    halves = []
    for s in range(2):
        total = jnp.zeros((parts * blocks, lanes // 2), jnp.float32)
        for r in range(share):
            left = cols_ref[pl.ds(s * share + r, parts * blocks, stride=2 * share), :]
            total = total + contract(left, rows[r], ((1,), (1,)))
        halves.append(total)
    both = jnp.concatenate(halves, axis=1).reshape(blocks, parts, lanes)
    for b in range(blocks):
        out_ref[:, b, :] = both[b]


def gram(own, other, cols, parts, blocks):
    n_slots, lanes = own.shape
    share = n_slots // (2 * parts)
    return pl.pallas_call(
        gram_kernel,
        in_specs=[VMEM, VMEM, VMEM],
        out_specs=VMEM,
        out_shape=jax.ShapeDtypeStruct((parts, blocks, 2 * 4 * parts), jnp.float32),
        scratch_shapes=[
            pltpu.VMEM((share, 4 * parts, lanes), jnp.float32),
            pltpu.VMEM((2, n_slots, lanes), jnp.float32),
        ],
        compiler_params=SMALL,
        name="gram",
    )(own, other, cols)


def finish_kernel(tasks_ref, terms_ref, out_ref):
    group = lax.axis_index(DP)
    n_y, n_z, seqs = 4, 4, out_ref.shape[2]
    total = jnp.sum(terms_ref[...], axis=0) * (1.0 / seqs)
    tasks = tasks_ref[...]
    lane = lax.broadcasted_iota(jnp.int32, tasks.shape, 1)
    own = jnp.sum(jnp.where(lane == group, tasks, 0), axis=1, keepdims=True)
    same = jnp.where(tasks == own, 1.0, 0.0)
    blocks = out_ref.shape[0]
    row = lax.broadcasted_iota(jnp.int32, (blocks, blocks), 0)
    col = lax.broadcasted_iota(jnp.int32, (blocks, blocks), 1)
    hit = row % n_z * n_y + row // n_z == col
    live = jnp.sum(jnp.where(hit, jnp.broadcast_to(same, (blocks, blocks)), 0.0), axis=1, keepdims=True)
    total = jnp.where(live > 0.5, total, 0.0)
    for y in range(n_y):
        for z in range(n_z):
            line = total[y * n_z + z : y * n_z + z + 1]
            out_ref[z * n_y + y] = jnp.concatenate([line[:, :seqs], line[:, seqs:]], axis=0)


def finish(tasks, terms):
    _, groups, lanes = terms.shape
    return pl.pallas_call(
        finish_kernel,
        in_specs=[VMEM, VMEM],
        out_specs=VMEM,
        out_shape=jax.ShapeDtypeStruct((groups, 2, lanes // 2), jnp.float32),
        compiler_params=SMALL,
        name="finish",
    )(tasks[None], terms)


def body(hidden, out_grad, proj_in, proj_out, lengths, task_ids):
    block_rows, seq_len, _ = hidden.shape
    rank = proj_in.shape[1]
    groups = lax.axis_size(DP)
    chips = lax.axis_size(CHIPS)
    share = block_rows // lax.axis_size(TENSOR)
    pair_rows = share * seq_len

    hidden = hidden.reshape(chips, 2, pair_rows, -1)
    out_grad = out_grad.reshape(chips, 2, pair_rows, -1)
    weights = (proj_in.T, proj_out.T)
    send = project(hidden, out_grad, *weights)
    keep = project_rest(hidden, out_grad, *weights)
    mine = add(keep, lax.ppermute(send, "core", [(0, 1), (1, 0)]))
    terms = exchange(mine, CHIPS)
    n_z = lax.axis_size("z_hi")
    units = sketches(lengths, terms, n_z)
    spread = exchange(units, ("z_hi",) + CHIPS).reshape(n_z, -1, 2 * rank)
    mine = lax.dynamic_index_in_dim(spread, lax.axis_index("z_hi"), 0, keepdims=False)
    other = lax.ppermute(mine, "core", [(0, 1), (1, 0)])
    cols = gather(spread, "y").reshape(-1, 2 * rank)
    partial_value = gram(mine, other, cols, chips, groups)
    return finish(task_ids, exchange(partial_value, CHIPS)).transpose(2, 0, 1)


def solution(mesh):
    fine = Mesh(np.asarray(mesh.devices).reshape(SIZES), AXES)
    in_specs = (
        P(DP, None, TENSOR),
        P(DP, None, TENSOR),
        P(TENSOR, None),
        P(TENSOR, None),
        P(DP),
        P(),
    )
    out_specs = P(DP, None, TENSOR)
    return jax.shard_map(body, mesh=fine, in_specs=in_specs, out_specs=out_specs, check_vma=False)
```

```python
import jax
import jax.numpy as jnp
import numpy as np
from jax import lax
from jax.experimental import pallas as pl
from jax.experimental.pallas import tpu as pltpu
from jax.sharding import Mesh
from jax.sharding import PartitionSpec as P

epsilon = 1e-06

AXES = ("z_hi", "y", "z_lo", "x", "core")
SIZES = (4, 4, 4, 4, 2)
DP = ("z_hi", "y")
TENSOR = ("z_lo", "x", "core")
CHIPS = ("z_lo", "x")

HIGHEST = lax.Precision.HIGHEST
VMEM = pl.BlockSpec(memory_space=pltpu.VMEM)
CHUNKS = 2
HBM = pl.BlockSpec(memory_space=pltpu.HBM)
SMALL = pltpu.CompilerParams(vmem_limit_bytes=8 * 1024 * 1024)


def contract(left, right, dims):
    return lax.dot_general(
        left, right, (dims, ((), ())), preferred_element_type=jnp.float32, precision=HIGHEST
    )


def exchange(value, axes):
    return lax.all_to_all(value, axes, 0, 0, tiled=True)


def gather(value, axis):
    copies = jnp.broadcast_to(value[None], (lax.axis_size(axis),) + value.shape)
    return exchange(copies, axis)


def project_kernel(hidden_hbm, grad_hbm, in_hbm, out_hbm, terms_ref, hidden, grad, w_in, w_out, sems):
    core = 1 - lax.axis_index("core")
    pairs, rows, lanes = terms_ref.shape
    block = pairs // CHUNKS
    dims = (((1,), (1,)), ((), ()))
    weights = [
        pltpu.make_async_copy(in_hbm, w_in, sems.at[0, CHUNKS]),
        pltpu.make_async_copy(out_hbm, w_out, sems.at[1, CHUNKS]),
    ]
    for copy in weights:
        copy.start()
    chunks = []
    for j in range(CHUNKS):
        span = pl.ds(j * block, block)
        chunks.append(
            [
                pltpu.make_async_copy(hidden_hbm.at[span, core], hidden.at[span], sems.at[0, j]),
                pltpu.make_async_copy(grad_hbm.at[span, core], grad.at[span], sems.at[1, j]),
            ]
        )
        for copy in chunks[-1]:
            copy.start()
    for copy in weights:
        copy.wait()
    for j in range(CHUNKS):
        for copy in chunks[j]:
            copy.wait()
        span = slice(j * block, (j + 1) * block)
        acts = hidden[span].reshape(block * rows, -1)
        grads = grad[span].reshape(block * rows, -1)
        left = lax.dot_general(acts, w_in[...], dims, preferred_element_type=jnp.float32)
        right = lax.dot_general(grads, w_out[...], dims, preferred_element_type=jnp.float32)
        terms_ref[span] = jnp.concatenate([left, right], axis=1).reshape(block, rows, lanes)


def project(hidden, grad, weights_in, weights_out):
    pairs, _, rows, wide = hidden.shape
    narrow = grad.shape[3]
    rank = weights_in.shape[0]
    operands = (hidden, grad, weights_in, weights_out)
    return pl.pallas_call(
        project_kernel,
        in_specs=[HBM, HBM, HBM, HBM],
        out_specs=VMEM,
        out_shape=jax.ShapeDtypeStruct((pairs, rows, 2 * rank), jnp.float32),
        scratch_shapes=[
            pltpu.VMEM((pairs, rows, wide), hidden.dtype),
            pltpu.VMEM((pairs, rows, narrow), grad.dtype),
            pltpu.VMEM(weights_in.shape, weights_in.dtype),
            pltpu.VMEM(weights_out.shape, weights_out.dtype),
            pltpu.SemaphoreType.DMA((2, CHUNKS + 1)),
        ],
        compiler_params=pltpu.CompilerParams(vmem_limit_bytes=16 * 1024 * 1024),
        cost_estimate=pl.CostEstimate(
            flops=2 * pairs * rows * rank * (wide + narrow),
            bytes_accessed=2 * pairs * rows * (wide + narrow) + 8 * pairs * rows * rank,
            transcendentals=0,
        ),
        name="project",
    )(*(pltpu.with_memory_space_constraint(v, pltpu.HBM) for v in operands))


def rest_kernel(hidden_ref, grad_ref, in_ref, out_ref, terms_ref):
    core = lax.axis_index("core")
    pairs, rows, lanes = terms_ref.shape
    block = pairs // CHUNKS
    dims = (((1,), (1,)), ((), ()))
    for j in range(CHUNKS):
        span = slice(j * block, (j + 1) * block)
        acts = hidden_ref[span, core].reshape(block * rows, -1)
        grads = grad_ref[span, core].reshape(block * rows, -1)
        left = lax.dot_general(acts, in_ref[...], dims, preferred_element_type=jnp.float32)
        right = lax.dot_general(grads, out_ref[...], dims, preferred_element_type=jnp.float32)
        terms_ref[span] = jnp.concatenate([left, right], axis=1).reshape(block, rows, lanes)


def project_rest(hidden, grad, weights_in, weights_out):
    pairs, _, rows, wide = hidden.shape
    rank = weights_in.shape[0]
    return pl.pallas_call(
        rest_kernel,
        in_specs=[VMEM, VMEM, VMEM, VMEM],
        out_specs=VMEM,
        out_shape=jax.ShapeDtypeStruct((pairs, rows, 2 * rank), jnp.float32),
        compiler_params=pltpu.CompilerParams(vmem_limit_bytes=16 * 1024 * 1024),
        cost_estimate=pl.CostEstimate(
            flops=2 * pairs * rows * rank * (wide + grad.shape[3]),
            bytes_accessed=8 * pairs * rows * rank,
            transcendentals=0,
        ),
        name="project_rest",
    )(hidden, grad, weights_in, weights_out)


def add_kernel(left_ref, right_ref, out_ref):
    out_ref[...] = left_ref[...] + right_ref[...]


def add(left, right):
    return pl.pallas_call(
        add_kernel,
        in_specs=[VMEM, VMEM],
        out_specs=VMEM,
        out_shape=jax.ShapeDtypeStruct(left.shape, left.dtype),
        compiler_params=SMALL,
        name="add",
    )(left, right)


def sketch_kernel(lengths_ref, terms_ref, out_ref):
    first = 2 * lax.axis_index(TENSOR)
    total = jnp.sum(terms_ref[...], axis=0)
    share = out_ref.shape[1] // 2
    parts = terms_ref.shape[0]
    copies = out_ref.shape[0] // parts
    seq_len, rank = total.shape[0] // 2, total.shape[1] // 2
    slot = lax.broadcasted_iota(jnp.int32, (seq_len, rank), 0)
    lengths = lengths_ref[...]
    lane = lax.broadcasted_iota(jnp.int32, lengths.shape, 1)
    for s in range(2):
        mine = total[s * seq_len : (s + 1) * seq_len]
        length = jnp.sum(jnp.where(lane == first + s, lengths, 0), axis=1, keepdims=True)
        live = (slot < length).astype(jnp.float32)
        sketch = contract(mine[:, :rank] * live, mine[:, rank:], ((0,), (0,)))
        mean = jnp.sum(sketch * sketch) / (rank * rank)
        unit = sketch / jnp.sqrt(jnp.full((1, 1), mean, jnp.float32) + epsilon)
        wide = jnp.concatenate([unit[: rank // 2], unit[rank // 2 :]], axis=1)
        for j in range(parts):
            piece = wide[j * share : (j + 1) * share]
            for k in range(copies):
                out_ref[k * parts + j, s * share : (s + 1) * share, :] = piece


def sketches(lengths, terms, copies):
    parts, slots, lanes = terms.shape
    rows = slots // (2 * parts)
    return pl.pallas_call(
        sketch_kernel,
        in_specs=[VMEM, VMEM],
        out_specs=VMEM,
        out_shape=jax.ShapeDtypeStruct((copies * parts, 2 * rows, lanes), jnp.float32),
        compiler_params=SMALL,
        name="sketches",
    )(lengths[None], terms)


def gram_kernel(own_ref, other_ref, cols_ref, out_ref, rows, held):
    parts, blocks, lanes = out_ref.shape
    share = rows.shape[0]
    first = lax.axis_index("core") == 0
    own, other = own_ref[...], other_ref[...]
    held[0] = jnp.where(first, own, other)
    held[1] = jnp.where(first, other, own)
    for core in range(2):
        for s in range(2):
            for r in range(share):
                rows[r, pl.ds(2 * core + s, parts, stride=4), :] = held[
                    core, pl.ds(s * share + r, parts, stride=2 * share), :
                ]
    halves = []
    for s in range(2):
        total = jnp.zeros((parts * blocks, lanes // 2), jnp.float32)
        for r in range(share):
            left = cols_ref[pl.ds(s * share + r, parts * blocks, stride=2 * share), :]
            total = total + contract(left, rows[r], ((1,), (1,)))
        halves.append(total)
    both = jnp.concatenate(halves, axis=1).reshape(blocks, parts, lanes)
    for b in range(blocks):
        out_ref[:, b, :] = both[b]


def gram(own, other, cols, parts, blocks):
    n_slots, lanes = own.shape
    share = n_slots // (2 * parts)
    return pl.pallas_call(
        gram_kernel,
        in_specs=[VMEM, VMEM, VMEM],
        out_specs=VMEM,
        out_shape=jax.ShapeDtypeStruct((parts, blocks, 2 * 4 * parts), jnp.float32),
        scratch_shapes=[
            pltpu.VMEM((share, 4 * parts, lanes), jnp.float32),
            pltpu.VMEM((2, n_slots, lanes), jnp.float32),
        ],
        compiler_params=SMALL,
        name="gram",
    )(own, other, cols)


def finish_kernel(tasks_ref, terms_ref, out_ref):
    group = lax.axis_index(DP)
    n_y, n_z, seqs = 4, 4, out_ref.shape[2]
    total = jnp.sum(terms_ref[...], axis=0) * (1.0 / seqs)
    tasks = tasks_ref[...]
    lane = lax.broadcasted_iota(jnp.int32, tasks.shape, 1)
    own = jnp.sum(jnp.where(lane == group, tasks, 0), axis=1, keepdims=True)
    same = jnp.where(tasks == own, 1.0, 0.0)
    blocks = out_ref.shape[0]
    row = lax.broadcasted_iota(jnp.int32, (blocks, blocks), 0)
    col = lax.broadcasted_iota(jnp.int32, (blocks, blocks), 1)
    hit = row % n_z * n_y + row // n_z == col
    live = jnp.sum(jnp.where(hit, jnp.broadcast_to(same, (blocks, blocks)), 0.0), axis=1, keepdims=True)
    total = jnp.where(live > 0.5, total, 0.0)
    halves = (total[:, :seqs], total[:, seqs:])
    for y in range(n_y):
        for z in range(n_z):
            line = y * n_z + z
            for s in range(2):
                out_ref[z * n_y + y, s : s + 1, :] = halves[s][line : line + 1]


def finish(tasks, terms):
    _, groups, lanes = terms.shape
    return pl.pallas_call(
        finish_kernel,
        in_specs=[VMEM, VMEM],
        out_specs=VMEM,
        out_shape=jax.ShapeDtypeStruct((groups, 2, lanes // 2), jnp.float32),
        compiler_params=SMALL,
        name="finish",
    )(tasks[None], terms)


def body(hidden, out_grad, proj_in, proj_out, lengths, task_ids):
    block_rows, seq_len, _ = hidden.shape
    rank = proj_in.shape[1]
    groups = lax.axis_size(DP)
    chips = lax.axis_size(CHIPS)
    share = block_rows // lax.axis_size(TENSOR)
    pair_rows = share * seq_len

    hidden = hidden.reshape(chips, 2, pair_rows, -1)
    out_grad = out_grad.reshape(chips, 2, pair_rows, -1)
    weights = (proj_in.T, proj_out.T)
    send = project(hidden, out_grad, *weights)
    keep = project_rest(hidden, out_grad, *weights)
    mine = add(keep, lax.ppermute(send, "core", [(0, 1), (1, 0)]))
    terms = exchange(mine, CHIPS)
    n_z = lax.axis_size("z_hi")
    units = sketches(lengths, terms, n_z)
    spread = exchange(units, ("z_hi",) + CHIPS).reshape(n_z, -1, 2 * rank)
    mine = lax.dynamic_index_in_dim(spread, lax.axis_index("z_hi"), 0, keepdims=False)
    other = lax.ppermute(mine, "core", [(0, 1), (1, 0)])
    cols = gather(spread, "y").reshape(-1, 2 * rank)
    partial_value = gram(mine, other, cols, chips, groups)
    return finish(task_ids, exchange(partial_value, CHIPS)).transpose(2, 0, 1)


def solution(mesh):
    fine = Mesh(np.asarray(mesh.devices).reshape(SIZES), AXES)
    in_specs = (
        P(DP, None, TENSOR),
        P(DP, None, TENSOR),
        P(TENSOR, None),
        P(TENSOR, None),
        P(DP),
        P(),
    )
    out_specs = P(DP, None, TENSOR)
    return jax.shard_map(body, mesh=fine, in_specs=in_specs, out_specs=out_specs, check_vma=False)
```
